32 devices in a mesh: span: 16 (over z, x, core), seq: 2 (over y).
Axes of the slice: x: 2, y: 2, z: 4, core: 2. Of those that a mesh axis runs over, the one named last changes fastest.
Arguments:
- tokens: bfloat16 [8192, 1024], P(('span', 'seq')), may hold values from -48 to 48
- w_qkv: bfloat16 [1024, 3072], P('span'), may hold values from -0.1875 to 0.1875
- w_out: bfloat16 [1024, 1024], replicated, may hold values from -0.1875 to 0.1875
- w_cross: bfloat16 [1024, 2048], replicated, may hold values from -0.1875 to 0.1875
- ln_gain: float32 [1024], replicated, may hold values from 0.5 to 1.5
- ln_bias: float32 [1024], replicated, may hold values from -3 to 3
- queries: bfloat16 [1024, 1024], replicated, may hold values from -144 to 144
Outputs:
- encoded: bfloat16 [8192, 1024], P(('span', 'seq'))
- cross_out: bfloat16 [1024, 1024], P('span')
The draws below stay inside these ranges and needn't reach their ends.
All inputs are finite; a program needn't handle non-finite values.
Results may differ from the reference program's by a relative error of at most 0.013.
The reference program's roundings to bfloat16 on the way count: a program that leaves them out, or rounds other values in their place, can miss the bound.
Values may be sent and summed in bfloat16 or wider, within the bound.
A program may use at most 128 MiB of HBM per device.

```python
import math
import jax
import jax.numpy as jnp
from jax import lax

D = 1024
H = 16
DH = 64
NQ = 1024
L = 512
SPANS = 16
TOKENS = 8192


def draw_tokens(key, part):
    values = jnp.clip(jax.random.normal(jax.random.fold_in(key, 11), (TOKENS, D), jnp.float32), -6.0, 6.0)
    return values.astype(jnp.bfloat16)


def draw_queries(key, part):
    query_scale = 43.6 / math.sqrt(DH)
    values = query_scale * jnp.clip(jax.random.normal(jax.random.fold_in(key, 23), (NQ, D), jnp.float32), -4.0, 4.0)
    return values.astype(jnp.bfloat16)


def block_scale(own_key, extent, shards, low, high):
    def one(position, parts):
        heights = jax.random.uniform(jax.random.fold_in(jax.random.fold_in(own_key, 6), position), (parts,), jnp.float32, low / len(shards), high / len(shards))
        return jnp.repeat(jnp.exp(heights), extent[position] // parts).reshape((-1,) + (1,) * (len(extent) - position - 1))

    factor_of = one(*shards[0])
    for cut in shards[1:]:
        factor_of = factor_of * one(*cut)
    return factor_of


def gaussian(own_key, extent, deviation, bound, pieces=(), dtype=jnp.bfloat16):
    result = jax.random.normal(own_key, extent, jnp.float32) * deviation
    if len(pieces) > 0:
        result = block_scale(own_key, extent, pieces, -0.22, 0.18) * result
    return jnp.clip(result, min=-bound, max=bound).astype(dtype)


def setup_inputs(seed: int = 0) -> dict:
    streams_of = jax.random.split(jax.random.key(seed), 8)
    tokens = draw_tokens(jax.random.fold_in(streams_of[7], 71), 0)
    w_qkv = gaussian(streams_of[1], (D, 3 * D), D ** -0.5, 0.1875, ((0, 16),))
    w_out = gaussian(streams_of[2], (D, D), D ** -0.5, 0.1875)
    w_cross = gaussian(streams_of[3], (D, 2 * D), D ** -0.5, 0.1875)
    ln_gain = jnp.clip(jax.random.uniform(streams_of[4], (D,), jnp.float32, 0.5, 1.5), 0.5, 1.5)
    ln_bias = gaussian(streams_of[5], (D,), 0.5, 3.0, (), jnp.float32)
    queries = draw_queries(jax.random.fold_in(streams_of[7], 71), 0)
    return dict(tokens=tokens, w_qkv=w_qkv, w_out=w_out, w_cross=w_cross, ln_gain=ln_gain, ln_bias=ln_bias, queries=queries)


score_scale = 0.125

def layer_norm(residual, ln_gain, ln_bias):
    center = residual - lax.optimization_barrier(jnp.mean(residual, -1, keepdims=True))
    spread = lax.optimization_barrier(jnp.mean(center * center, -1, keepdims=True))
    return center * lax.rsqrt(spread + 1e-05) * ln_gain + ln_bias

def head_attend(triple):
    scores = jnp.dot(triple[0], triple[1].T, preferred_element_type=jnp.float32) * score_scale
    peaks = lax.optimization_barrier(jnp.max(scores, -1, keepdims=True))
    powers = jnp.exp(scores - peaks)
    totals = lax.optimization_barrier(jnp.sum(powers, -1, keepdims=True))
    return (jnp.dot(powers.astype(jnp.bfloat16), triple[2], preferred_element_type=jnp.float32) / totals).astype(jnp.bfloat16)

def reference(tokens, w_qkv, w_out, w_cross, ln_gain, ln_bias, queries):

    def encode_span(span_tokens):
        projected = jnp.dot(span_tokens, w_qkv, preferred_element_type=jnp.float32).astype(jnp.bfloat16)
        per_head = jnp.transpose(projected.reshape(L, 3, H, DH), (2, 1, 0, 3))
        head_outputs = lax.map(lambda triple: head_attend((triple[0], triple[1], triple[2])), per_head)
        attn = jnp.transpose(head_outputs, (1, 0, 2)).reshape(L, D)
        residual = span_tokens.astype(jnp.float32) + jnp.dot(attn, w_out, preferred_element_type=jnp.float32)
        encoded = layer_norm(residual, ln_gain, ln_bias).astype(jnp.bfloat16)
        cross_kv = jnp.dot(encoded, w_cross, preferred_element_type=jnp.float32).astype(jnp.bfloat16)
        return (encoded, cross_kv)
    encoded, cross_kv = lax.map(encode_span, tokens.reshape(SPANS, L, D))
    cross_kv = cross_kv.reshape(TOKENS, 2 * D)
    key_heads = jnp.transpose(cross_kv[:, :D].reshape(TOKENS, H, DH), (1, 0, 2))
    value_heads = jnp.transpose(cross_kv[:, D:].reshape(TOKENS, H, DH), (1, 0, 2))
    query_heads = jnp.transpose(queries.reshape(NQ, H, DH), (1, 0, 2))
    cross_heads = lax.map(lambda triple: head_attend((triple[0], triple[1], triple[2])), (query_heads, key_heads, value_heads))
    cross_out = jnp.transpose(cross_heads, (1, 0, 2)).reshape(NQ, D)
    return (encoded.reshape(TOKENS, D), cross_out)
```

```python
import functools

import jax
import jax.numpy as jnp
from jax import lax
from jax.experimental import pallas as pl
from jax.experimental.pallas import tpu as pltpu
from jax.sharding import PartitionSpec as P

DH = 64
PAIR = 2 * DH
score_scale = 0.125
F32 = jnp.float32
BF16 = jnp.bfloat16
MESH = pl.DeviceIdType.MESH


def mm(a, b):
    return jnp.dot(a, b, preferred_element_type=F32)


def mm_t(a, b):
    return lax.dot_general(a, b, (((1,), (1,)), ((), ())), preferred_element_type=F32)


def pair_attend(query, key, value):
    lane = lax.broadcasted_iota(jnp.int32, (1, PAIR), 1)
    low = lane < DH
    low_f = jnp.where(low, 1.0, 0.0)
    low_b = low_f.astype(BF16)
    high_b = (1.0 - low_f).astype(BF16)
    scaled = query * jnp.asarray(score_scale, BF16)

    def one(own, other):
        scores = mm_t(scaled * own, key)
        peak = jnp.max(scores, -1, keepdims=True)
        probs = jnp.exp(scores - peak).astype(BF16)
        return mm(probs, value * own + other), peak

    first, first_peak = one(low_b, high_b)
    second, second_peak = one(high_b, low_b)
    numerator = jnp.where(low, first, second)
    total = pltpu.roll(jnp.where(low, second, first), DH, 1)
    return numerator, total, jnp.where(low, first_peak, second_peak)


def kernel(
    S, Q, NQ,
    tokens_ref, wqkv_ref, wout_ref, wcross_ref, gain_ref, bias_ref, queries_ref,
    enc_ref, out_ref,
    wbuf, tokall, acc, qkv, wout, wc, qc, attn_tx, attn, res, kv_tx, kv, o_tx, l_tx, o_rx, l_rx,
    local_sem, z_send, z_recv, x_send, x_recv, c_send, c_recv,
    tok_send, tok_recv, at_send, at_recv, kv_send, kv_recv, o_send, o_recv, l_send, l_recv,
):
    T, D = tokens_ref.shape
    R = wqkv_ref.shape[0]
    hcols = D // Q
    Z = S // 4
    G = D // PAIR
    own_rows = NQ // S
    span = lax.axis_index("span")
    seq = lax.axis_index("seq")
    z = span // 4
    x = (span // 2) % 2
    c = span % 2
    member = span % G
    base = span - member
    flat = span * Q + seq

    loads = []

    def load(src, dst):
        copy = pltpu.make_async_copy(src, dst, local_sem.at[len(loads)])
        copy.start()
        loads.append(copy)
        return copy

    own_w = pl.ds(pl.multiple_of(span * R, R), R)
    w_loads = [
        load(
            wqkv_ref.at[:, pl.ds(pl.multiple_of(j * D + seq * hcols, 128), hcols)],
            wbuf.at[own_w, pl.ds(j * hcols, hcols)],
        )
        for j in range(3)
    ]
    own_t = pl.ds(pl.multiple_of(seq * T, T), T)
    t_load = load(tokens_ref, tokall.at[own_t])

    barrier = pltpu.get_barrier_semaphore()
    n = S * Q

    def greet(i, carry):
        other = (flat + i) % n
        pl.semaphore_signal(
            barrier, inc=1, device_id={"span": other // Q, "seq": other % Q}, device_id_type=MESH
        )
        return carry

    lax.fori_loop(1, n, greet, 0)
    wo_load = load(wout_ref, wout)
    wc_loads = []
    for g in range(G):
        for half in range(2):
            wc_loads.append(
                load(
                    wcross_ref.at[:, pl.ds(half * D + g * PAIR, PAIR)],
                    wc.at[g, :, pl.ds(half * PAIR, PAIR)],
                )
            )
    q_load = load(queries_ref.at[:, pl.ds(pl.multiple_of(member * PAIR, PAIR), PAIR)], qc)
    for copy in w_loads:
        copy.wait()
    pl.semaphore_wait(barrier, n - 1)

    def remote(src, dst, ssem, rsem, to_span, to_seq):
        return pltpu.make_async_remote_copy(
            src_ref=src, dst_ref=dst, send_sem=ssem, recv_sem=rsem,
            device_id={"span": to_span, "seq": to_seq}, device_id_type=MESH,
        )

    def block(zz, xx, cc):
        return wbuf.at[pl.ds(pl.multiple_of((zz * 4 + xx * 2 + cc) * R, R), R)]

    x_peer = z * 4 + (1 - x) * 2 + c
    c_peer = z * 4 + x * 2 + (1 - c)
    sent = []

    def send(copy):
        copy.start()
        sent.append(copy)

    def to_x(zz):
        b = block(zz, x, c)
        return remote(b, b, x_send.at[zz], x_recv.at[zz], x_peer, seq)

    def from_x(zz):
        b = block(zz, 1 - x, c)
        return remote(b, b, x_send.at[zz], x_recv.at[zz], x_peer, seq)

    def to_c(zz, xx):
        b = block(zz, xx, c)
        return remote(b, b, c_send.at[zz * 2 + xx], c_recv.at[zz * 2 + xx], c_peer, seq)

    def from_c(zz, xx):
        b = block(zz, xx, 1 - c)
        return remote(b, b, c_send.at[zz * 2 + xx], c_recv.at[zz * 2 + xx], c_peer, seq)

    def at_z(k):
        return (z + k) % Z

    order = [0]
    for d in range(1, Z // 2 + 1):
        for k in (d, Z - d):
            if k not in order:
                order.append(k)
    send(to_x(z))
    send(to_c(z, x))
    for k in order[1:]:
        b = block(z, x, c)
        send(remote(b, b, z_send.at[k], z_recv.at[z], at_z(k) * 4 + x * 2 + c, seq))
    t_load.wait()
    for j in range(1, Q):
        mine = tokall.at[own_t]
        send(remote(mine, mine, tok_send.at[j], tok_recv.at[seq], span, (seq + j) % Q))

    def project(step):
        zz = at_z(order[step])
        rows = pl.ds(pl.multiple_of(zz * 4 * R, 4 * R), 4 * R)
        for xx in range(2):
            from_c(zz, xx).wait_recv()

        def tile(i, carry):
            j = i // Q
            trows = pl.ds(pl.multiple_of((i % Q) * T, T), T)
            part = mm(
                tokall[trows, rows], wbuf[rows, pl.ds(pl.multiple_of(j * hcols, 128), hcols)]
            )
            if step == 0:
                acc[j, trows] = part
            elif step == Z - 1:
                qkv[j, trows] = (acc[j, trows] + part).astype(BF16)
            else:
                acc[j, trows] += part
            return carry

        lax.fori_loop(0, 3 * Q, tile, 0)

    for step in range(Z):
        if step + 1 < Z:
            zn = at_z(order[step + 1])
            b = block(zn, x, c)
            remote(b, b, z_send.at[1], z_recv.at[zn], zn * 4 + x * 2 + c, seq).wait_recv()
            send(to_x(zn))
            send(to_c(zn, x))
        zz = at_z(order[step])
        from_x(zz).wait_recv()
        send(to_c(zz, 1 - x))
        if step == 1:
            for j in range(1, Q):
                theirs = tokall.at[pl.ds(pl.multiple_of(((seq + j) % Q) * T, T), T)]
                remote(
                    theirs, theirs, tok_send.at[j], tok_recv.at[(seq + j) % Q], span, (seq + j) % Q
                ).wait_recv()
        if step >= 1:
            project(step - 1)
    project(Z - 1)

    def self_attend(owner, target):
        trows = pl.ds(pl.multiple_of(owner * T, T), T)

        def pair(p, carry):
            cols = pl.ds(pl.multiple_of(p * PAIR, PAIR), PAIR)
            num, tot, _ = pair_attend(qkv[0, trows, cols], qkv[1, :, cols], qkv[2, :, cols])
            target[:, cols] = (num / tot).astype(BF16)
            return carry

        lax.fori_loop(0, hcols // PAIR, pair, 0)

    for j in range(1, Q):
        owner = (seq + j) % Q
        self_attend(owner, attn_tx.at[j])
        send(remote(attn_tx.at[j], attn.at[seq], at_send.at[j], at_recv.at[seq], span, owner))
    self_attend(seq, attn.at[seq])
    wo_load.wait()
    NT = 256

    def out_part(j_seq, first):
        wrows = pl.ds(pl.multiple_of(j_seq * hcols, hcols), hcols)

        def tile(i, carry):
            cols = pl.ds(pl.multiple_of(i * NT, NT), NT)
            part = mm(attn[j_seq], wout[wrows, cols])
            if first:
                res[:, cols] = tokall[own_t, cols].astype(F32) + part
            else:
                res[:, cols] += part
            return carry

        lax.fori_loop(0, D // NT, tile, 0)

    out_part(seq, True)
    for j in range(1, Q):
        owner = (seq + j) % Q
        remote(
            attn_tx.at[j], attn.at[owner], at_send.at[j], at_recv.at[owner], span, owner
        ).wait_recv()
        out_part(owner, False)
    LT = 64

    def norm(i, carry):
        rows = pl.ds(pl.multiple_of(i * LT, LT), LT)
        r = res[rows]
        center = r - jnp.mean(r, -1, keepdims=True)
        spread = jnp.mean(center * center, -1, keepdims=True)
        enc_ref[rows] = (
            center * lax.rsqrt(spread + 1e-05) * gain_ref[...] + bias_ref[...]
        ).astype(BF16)
        return carry

    lax.fori_loop(0, T // LT, norm, 0)

    for copy in wc_loads:
        copy.wait()

    def kv_copy(g, at):
        return remote(
            kv_tx.at[g], kv.at[pl.ds(pl.multiple_of(at * T, T), T)],
            kv_send.at[g], kv_recv.at[at], base + g, seq,
        )

    def kv_step(i, carry):
        g = (member + i) % G
        kv_tx[g] = mm(enc_ref[...], wc[g]).astype(BF16)
        kv_copy(g, member).start()
        return carry

    lax.fori_loop(1, G, kv_step, 0)
    kv[pl.ds(pl.multiple_of(member * T, T), T)] = mm(enc_ref[...], wc[member]).astype(BF16)
    q_load.wait()

    def kv_wait(i, carry):
        g = (member + i) % G
        kv_copy(g, g).wait_recv()
        return carry

    lax.fori_loop(1, G, kv_wait, 0)

    BQ = max(own_rows, min(256, NQ))
    nb = BQ // own_rows
    lane = lax.broadcasted_iota(jnp.int32, (own_rows, PAIR), 1)
    row = lax.broadcasted_iota(jnp.int32, (own_rows, PAIR), 0)
    diagonal = (lane % DH) == row

    def part_copies(r, s):
        to = r * Q + s
        return (
            remote(o_tx.at[r], o_rx.at[flat], o_send.at[to], o_recv.at[flat], r, s),
            remote(l_tx.at[r], l_rx.at[flat], l_send.at[to], l_recv.at[flat], r, s),
        )

    def cross(i, carry):
        rows = pl.ds(pl.multiple_of(i * BQ, BQ), BQ)
        num, tot, peak = pair_attend(qc[rows], kv[:, :PAIR], kv[:, PAIR:])
        part = (num / tot).astype(BF16)
        lse = peak + jnp.log(tot)
        for b in range(nb):
            r = i * nb + b
            stat = jnp.sum(
                jnp.where(diagonal, lse[b * own_rows:(b + 1) * own_rows], 0.0), 0, keepdims=True
            )
            stat = jnp.broadcast_to(stat, (8, PAIR))
            o_tx[r] = part[b * own_rows:(b + 1) * own_rows]
            l_tx[r] = stat

            @pl.when(r == span)
            def _():
                o_rx[flat] = part[b * own_rows:(b + 1) * own_rows]
                l_rx[flat] = stat

            for s in range(Q):
                @pl.when(r * Q + s != flat)
                def _():
                    for copy in part_copies(r, s):
                        copy.start()
        return carry

    lax.fori_loop(0, NQ // BQ, cross, 0)

    def part_wait(i, carry):
        src = (flat + i) % n
        r = src // Q
        s = src % Q
        remote(o_tx.at[r], o_rx.at[src], o_send.at[src], o_recv.at[src], r, s).wait_recv()
        remote(l_tx.at[r], l_rx.at[src], l_send.at[src], l_recv.at[src], r, s).wait_recv()
        return carry

    lax.fori_loop(1, n, part_wait, 0)

    low = lane < DH

    def merge(g, carry):
        sources = [(a * G + g) * Q + s for a in range(S // G) for s in range(Q)]
        stats = [l_rx[src][0:1] for src in sources]
        top = functools.reduce(jnp.maximum, stats)
        weights = [jnp.exp(v - top) for v in stats]
        whole = functools.reduce(jnp.add, weights)
        total = jnp.zeros((own_rows, PAIR), F32)
        for src, weight in zip(sources, weights):
            spread = jnp.where(diagonal, weight / whole, 0.0)
            left = jnp.sum(jnp.where(low, spread, 0.0), 1, keepdims=True)
            right = jnp.sum(jnp.where(low, 0.0, spread), 1, keepdims=True)
            total += o_rx[src].astype(F32) * jnp.where(low, left, right)
        out_ref[:, pl.ds(pl.multiple_of(g * PAIR, PAIR), PAIR)] = total.astype(BF16)
        return carry

    lax.fori_loop(0, G, merge, 0)

    for copy in sent:
        copy.wait_send()

    def kv_sent(i, carry):
        kv_copy((member + i) % G, member).wait_send()
        return carry

    lax.fori_loop(1, G, kv_sent, 0)

    def part_sent(i, carry):
        to = (flat + i) % n
        for copy in part_copies(to // Q, to % Q):
            copy.wait_send()
        return carry

    lax.fori_loop(1, n, part_sent, 0)


def solution(mesh):
    S = mesh.shape["span"]
    Q = mesh.shape["seq"]

    def per_device(tokens, w_qkv, w_out, w_cross, ln_gain, ln_bias, queries):
        T, D = tokens.shape
        NQ = queries.shape[0]
        hcols = D // Q
        Z = S // 4
        G = D // PAIR
        own_rows = NQ // S
        any_spec = pl.BlockSpec(memory_space=pl.ANY)
        vmem_spec = pl.BlockSpec(memory_space=pltpu.VMEM)
        dma = pltpu.SemaphoreType.DMA
        n = S * Q
        return pl.pallas_call(
            functools.partial(kernel, S, Q, NQ),
            out_shape=(
                jax.ShapeDtypeStruct((T, D), BF16),
                jax.ShapeDtypeStruct((own_rows, D), BF16),
            ),
            in_specs=[any_spec] * 4 + [vmem_spec] * 2 + [any_spec],
            out_specs=(vmem_spec, vmem_spec),
            scratch_shapes=[
                pltpu.VMEM((D, 3 * hcols), BF16),
                pltpu.VMEM((Q * T, D), BF16),
                pltpu.VMEM((3, Q * T, hcols), F32),
                pltpu.VMEM((3, Q * T, hcols), BF16),
                pltpu.VMEM((D, D), BF16),
                pltpu.VMEM((G, D, 2 * PAIR), BF16),
                pltpu.VMEM((NQ, PAIR), BF16),
                pltpu.VMEM((Q, T, hcols), BF16),
                pltpu.VMEM((Q, T, hcols), BF16),
                pltpu.VMEM((T, D), F32),
                pltpu.VMEM((G, T, 2 * PAIR), BF16),
                pltpu.VMEM((G * T, 2 * PAIR), BF16),
                pltpu.VMEM((S, own_rows, PAIR), BF16),
                pltpu.VMEM((S, 8, PAIR), F32),
                pltpu.VMEM((n, own_rows, PAIR), BF16),
                pltpu.VMEM((n, 8, PAIR), F32),
                dma((6 + 2 * G,)),
                dma((Z,)), dma((Z,)), dma((Z,)), dma((Z,)), dma((2 * Z,)), dma((2 * Z,)),
                dma((Q,)), dma((Q,)), dma((Q,)), dma((Q,)), dma((G,)), dma((G,)),
                dma((n,)), dma((n,)), dma((n,)), dma((n,)),
            ],
            compiler_params=pltpu.CompilerParams(
                collective_id=0, has_side_effects=True, vmem_limit_bytes=56 << 20
            ),
        )(tokens, w_qkv, w_out, w_cross, ln_gain.reshape(1, D), ln_bias.reshape(1, D), queries)

    in_specs = (P(("span", "seq"), None), P("span", None), P(), P(), P(), P(), P())
    out_specs = (P(("span", "seq"), None), P("span", None))
    return jax.shard_map(
        per_device, mesh=mesh, in_specs=in_specs, out_specs=out_specs, check_vma=False
    )
```

```python
import functools

import jax
import jax.numpy as jnp
from jax import lax
from jax.experimental import pallas as pl
from jax.experimental.pallas import tpu as pltpu
from jax.sharding import PartitionSpec as P

DH = 64
PAIR = 2 * DH
score_scale = 0.125
F32 = jnp.float32
BF16 = jnp.bfloat16
MESH = pl.DeviceIdType.MESH


def mm(a, b):
    return jnp.dot(a, b, preferred_element_type=F32)


def mm_t(a, b):
    return lax.dot_general(a, b, (((1,), (1,)), ((), ())), preferred_element_type=F32)


def pair_attend(query, key, value):
    lane = lax.broadcasted_iota(jnp.int32, (1, PAIR), 1)
    low = lane < DH
    low_f = jnp.where(low, 1.0, 0.0)
    low_b = low_f.astype(BF16)
    high_b = (1.0 - low_f).astype(BF16)
    scaled = query * jnp.asarray(score_scale, BF16)

    def one(own, other):
        scores = mm_t(scaled * own, key)
        peak = jnp.max(scores, -1, keepdims=True)
        probs = jnp.exp(scores - peak).astype(BF16)
        return mm(probs, value * own + other), peak

    first, first_peak = one(low_b, high_b)
    second, second_peak = one(high_b, low_b)
    numerator = jnp.where(low, first, second)
    total = pltpu.roll(jnp.where(low, second, first), DH, 1)
    return numerator, total, jnp.where(low, first_peak, second_peak)


def kernel(
    S, Q, NQ,
    tokens_ref, wqkv_ref, wout_ref, wcross_ref, gain_ref, bias_ref, queries_ref,
    enc_ref, out_ref,
    wbuf, tokall, acc, qkv, wout, wc, qc, attn_tx, attn, res, kv_tx, kv, o_tx, l_tx, o_rx, l_rx,
    local_sem, r_send, l_out, z_recv, x_send, x_recv, c_send, c_recv,
    tok_send, tok_recv, at_send, at_recv, kv_send, kv_recv, o_send, o_recv, l_send, l_recv,
):
    T, D = tokens_ref.shape
    R = wqkv_ref.shape[0]
    hcols = D // Q
    Z = S // 4
    G = D // PAIR
    own_rows = NQ // S
    span = lax.axis_index("span")
    seq = lax.axis_index("seq")
    z = span // 4
    x = (span // 2) % 2
    c = span % 2
    member = span % G
    base = span - member
    flat = span * Q + seq

    loads = []

    def load(src, dst):
        copy = pltpu.make_async_copy(src, dst, local_sem.at[len(loads)])
        copy.start()
        loads.append(copy)
        return copy

    own_w = pl.ds(pl.multiple_of(span * R, R), R)
    w_loads = [
        load(
            wqkv_ref.at[:, pl.ds(pl.multiple_of(j * D + seq * hcols, 128), hcols)],
            wbuf.at[own_w, pl.ds(j * hcols, hcols)],
        )
        for j in range(3)
    ]
    own_t = pl.ds(pl.multiple_of(seq * T, T), T)
    t_load = load(tokens_ref, tokall.at[own_t])

    barrier = pltpu.get_barrier_semaphore()
    n = S * Q

    def greet(to_span, to_seq):
        pl.semaphore_signal(
            barrier, inc=1, device_id={"span": to_span, "seq": to_seq}, device_id_type=MESH
        )

    x_peer = z * 4 + (1 - x) * 2 + c
    c_peer = z * 4 + x * 2 + (1 - c)
    greet(c_peer, seq)
    greet(x_peer, seq)
    for j in range(1, Q):
        greet(span, (seq + j) % Q)
    has_right = z < Z - 1
    has_left = z > 0

    @pl.when(has_right)
    def _():
        greet(span + 4, seq)

    @pl.when(has_left)
    def _():
        greet(span - 4, seq)

    wo_load = load(wout_ref, wout)
    wc_loads = []
    for g in range(G):
        for half in range(2):
            wc_loads.append(
                load(
                    wcross_ref.at[:, pl.ds(half * D + g * PAIR, PAIR)],
                    wc.at[g, :, pl.ds(half * PAIR, PAIR)],
                )
            )
    q_load = load(queries_ref.at[:, pl.ds(pl.multiple_of(member * PAIR, PAIR), PAIR)], qc)
    for copy in w_loads:
        copy.wait()
    sides = (z + Z - 2) // (Z - 1) + (2 * Z - 3 - z) // (Z - 1)
    pl.semaphore_wait(barrier, Q + 1 + sides)

    def remote(src, dst, ssem, rsem, to_span, to_seq):
        return pltpu.make_async_remote_copy(
            src_ref=src, dst_ref=dst, send_sem=ssem, recv_sem=rsem,
            device_id={"span": to_span, "seq": to_seq}, device_id_type=MESH,
        )

    def block(zz, xx, cc):
        return wbuf.at[pl.ds(pl.multiple_of((zz * 4 + xx * 2 + cc) * R, R), R)]

    sent = []

    def send(copy):
        copy.start()
        sent.append(copy)

    def by_x(zz, xx):
        b = block(zz, xx, c)
        return remote(b, b, x_send.at[zz], x_recv.at[zz], x_peer, seq)

    def by_c(zz, xx, cc):
        b = block(zz, xx, cc)
        return remote(b, b, c_send.at[zz * 2 + xx], c_recv.at[zz * 2 + xx], c_peer, seq)

    def by_right(zz):
        b = block(zz, x, c)
        return remote(b, b, r_send.at[zz], z_recv.at[zz], span + 4, seq)

    def by_left(zz):
        b = block(zz, x, c)
        return remote(b, b, l_out.at[zz], z_recv.at[zz], span - 4, seq)

    def spread(zz, rightward, leftward):
        if rightward:
            @pl.when(has_right)
            def _():
                by_right(zz).start()
        if leftward:
            @pl.when(has_left)
            def _():
                by_left(zz).start()
        by_x(zz, x).start()
        by_c(zz, x, c).start()

    def cross_over(zz):
        by_x(zz, 1 - x).wait_recv()
        by_c(zz, 1 - x, c).start()

    def project(zz, first):
        rows = pl.ds(pl.multiple_of(zz * 4 * R, 4 * R), 4 * R)
        for xx in range(2):
            by_c(zz, xx, 1 - c).wait_recv()

        def tile(i, carry):
            j = i // Q
            trows = pl.ds(pl.multiple_of((i % Q) * T, T), T)
            part = mm(
                tokall[trows, rows], wbuf[rows, pl.ds(pl.multiple_of(j * hcols, 128), hcols)]
            )
            if first:
                acc[j, trows] = part
            else:
                acc[j, trows] += part
            return carry

        lax.fori_loop(0, 3 * Q, tile, 0)

    spread(z, True, True)
    t_load.wait()
    for j in range(1, Q):
        mine = tokall.at[own_t]
        send(remote(mine, mine, tok_send.at[j], tok_recv.at[seq], span, (seq + j) % Q))

    def at_distance(t, action):
        @pl.when(z >= t)
        def _():
            action(z - t, True)

        @pl.when(z + t < Z)
        def _():
            action(z + t, False)

    def arrive(zz, from_left):
        by_right(zz).wait_recv()
        spread(zz, from_left, not from_left)

    for t in range(Z):
        if t + 1 < Z:
            at_distance(t + 1, arrive)
        if t == 0:
            cross_over(z)
        else:
            at_distance(t, lambda zz, _: cross_over(zz))
        if t == 1:
            for j in range(1, Q):
                theirs = tokall.at[pl.ds(pl.multiple_of(((seq + j) % Q) * T, T), T)]
                remote(
                    theirs, theirs, tok_send.at[j], tok_recv.at[(seq + j) % Q], span, (seq + j) % Q
                ).wait_recv()
            project(z, True)
        elif t > 1:
            at_distance(t - 1, lambda zz, _: project(zz, False))
    at_distance(Z - 1, lambda zz, _: project(zz, False))

    def round_off(i, carry):
        j = i // Q
        trows = pl.ds(pl.multiple_of((i % Q) * T, T), T)
        qkv[j, trows] = acc[j, trows].astype(BF16)
        return carry

    lax.fori_loop(0, 3 * Q, round_off, 0)

    def pair_copy(j, p, at, owner):
        cols = pl.ds(pl.multiple_of(p * PAIR, PAIR), PAIR)
        return remote(
            attn_tx.at[j, :, cols], attn.at[at, :, cols], at_send.at[j, p], at_recv.at[at, p],
            span, owner,
        )

    def self_attend(j, owner, target):
        trows = pl.ds(pl.multiple_of(owner * T, T), T)

        def pair(p, carry):
            cols = pl.ds(pl.multiple_of(p * PAIR, PAIR), PAIR)
            num, tot, _ = pair_attend(qkv[0, trows, cols], qkv[1, :, cols], qkv[2, :, cols])
            target[:, cols] = (num / tot).astype(BF16)
            if j:
                pair_copy(j, p, seq, owner).start()
            return carry

        lax.fori_loop(0, hcols // PAIR, pair, 0)

    for j in range(1, Q):
        owner = (seq + j) % Q
        self_attend(j, owner, attn_tx.at[j])
    self_attend(0, seq, attn.at[seq])
    wo_load.wait()
    NT = 256

    def out_part(j_seq, first):
        wrows = pl.ds(pl.multiple_of(j_seq * hcols, hcols), hcols)

        def tile(i, carry):
            cols = pl.ds(pl.multiple_of(i * NT, NT), NT)
            part = mm(attn[j_seq], wout[wrows, cols])
            if first:
                res[:, cols] = tokall[own_t, cols].astype(F32) + part
            else:
                res[:, cols] += part
            return carry

        lax.fori_loop(0, D // NT, tile, 0)

    out_part(seq, True)
    for j in range(1, Q):
        owner = (seq + j) % Q
        for p in range(hcols // PAIR):
            pair_copy(j, p, owner, owner).wait_recv()
        out_part(owner, False)
    LT = 64

    def norm(i, carry):
        rows = pl.ds(pl.multiple_of(i * LT, LT), LT)
        r = res[rows]
        center = r - jnp.mean(r, -1, keepdims=True)
        spread = jnp.mean(center * center, -1, keepdims=True)
        enc_ref[rows] = (
            center * lax.rsqrt(spread + 1e-05) * gain_ref[...] + bias_ref[...]
        ).astype(BF16)
        return carry

    lax.fori_loop(0, T // LT, norm, 0)

    for copy in wc_loads:
        copy.wait()

    def kv_copy(g, at):
        return remote(
            kv_tx.at[g], kv.at[pl.ds(pl.multiple_of(at * T, T), T)],
            kv_send.at[g], kv_recv.at[at], base + g, seq,
        )

    def kv_step(i, carry):
        g = (member + i) % G
        kv_tx[g] = mm(enc_ref[...], wc[g]).astype(BF16)
        kv_copy(g, member).start()
        return carry

    lax.fori_loop(1, G, kv_step, 0)
    kv[pl.ds(pl.multiple_of(member * T, T), T)] = mm(enc_ref[...], wc[member]).astype(BF16)
    q_load.wait()

    def kv_wait(i, carry):
        g = (member + i) % G
        kv_copy(g, g).wait_recv()
        return carry

    lax.fori_loop(1, G, kv_wait, 0)

    BQ = max(own_rows, min(256, NQ))
    nb = BQ // own_rows
    lane = lax.broadcasted_iota(jnp.int32, (own_rows, PAIR), 1)
    row = lax.broadcasted_iota(jnp.int32, (own_rows, PAIR), 0)
    diagonal = (lane % DH) == row

    def part_copies(r, s):
        to = r * Q + s
        return (
            remote(o_tx.at[r], o_rx.at[flat], o_send.at[to], o_recv.at[flat], r, s),
            remote(l_tx.at[r], l_rx.at[flat], l_send.at[to], l_recv.at[flat], r, s),
        )

    def cross(step, carry):
        i = (z + 1 + step) % (NQ // BQ)
        rows = pl.ds(pl.multiple_of(i * BQ, BQ), BQ)
        num, tot, peak = pair_attend(qc[rows], kv[:, :PAIR], kv[:, PAIR:])
        part = (num / tot).astype(BF16)
        lse = peak + jnp.log(tot)
        for b in range(nb):
            r = i * nb + b
            stat = jnp.sum(
                jnp.where(diagonal, lse[b * own_rows:(b + 1) * own_rows], 0.0), 0, keepdims=True
            )
            stat = jnp.broadcast_to(stat, (8, PAIR))
            o_tx[r] = part[b * own_rows:(b + 1) * own_rows]
            l_tx[r] = stat

            @pl.when(r == span)
            def _():
                o_rx[flat] = part[b * own_rows:(b + 1) * own_rows]
                l_rx[flat] = stat

            for s in range(Q):
                @pl.when(r * Q + s != flat)
                def _():
                    for copy in part_copies(r, s):
                        copy.start()
        return carry

    lax.fori_loop(0, NQ // BQ, cross, 0)

    def part_wait(i, carry):
        src = (flat + i) % n
        r = src // Q
        s = src % Q
        remote(o_tx.at[r], o_rx.at[src], o_send.at[src], o_recv.at[src], r, s).wait_recv()
        remote(l_tx.at[r], l_rx.at[src], l_send.at[src], l_recv.at[src], r, s).wait_recv()
        return carry

    lax.fori_loop(1, n, part_wait, 0)

    low = lane < DH

    def merge(g, carry):
        sources = [(a * G + g) * Q + s for a in range(S // G) for s in range(Q)]
        stats = [l_rx[src][0:1] for src in sources]
        top = functools.reduce(jnp.maximum, stats)
        weights = [jnp.exp(v - top) for v in stats]
        whole = functools.reduce(jnp.add, weights)
        total = jnp.zeros((own_rows, PAIR), F32)
        for src, weight in zip(sources, weights):
            spread = jnp.where(diagonal, weight / whole, 0.0)
            left = jnp.sum(jnp.where(low, spread, 0.0), 1, keepdims=True)
            right = jnp.sum(jnp.where(low, 0.0, spread), 1, keepdims=True)
            total += o_rx[src].astype(F32) * jnp.where(low, left, right)
        out_ref[:, pl.ds(pl.multiple_of(g * PAIR, PAIR), PAIR)] = total.astype(BF16)
        return carry

    lax.fori_loop(0, G, merge, 0)

    for copy in sent:
        copy.wait_send()
    for j in range(1, Q):
        for p in range(hcols // PAIR):
            pair_copy(j, p, seq, (seq + j) % Q).wait_send()
    for zz in range(Z):
        by_x(zz, x).wait_send()
        for xx in range(2):
            by_c(zz, xx, c).wait_send()

        @pl.when(has_right & (z >= zz))
        def _():
            by_right(zz).wait_send()

        @pl.when(has_left & (z <= zz))
        def _():
            by_left(zz).wait_send()

    def kv_sent(i, carry):
        kv_copy((member + i) % G, member).wait_send()
        return carry

    lax.fori_loop(1, G, kv_sent, 0)

    def part_sent(i, carry):
        to = (flat + i) % n
        for copy in part_copies(to // Q, to % Q):
            copy.wait_send()
        return carry

    lax.fori_loop(1, n, part_sent, 0)


def hand_over(enc_ref, part_ref, enc_out, part_out):
    enc_out[...] = enc_ref[...]
    part_out[...] = part_ref[...]


def solution(mesh):
    S = mesh.shape["span"]
    Q = mesh.shape["seq"]

    def per_device(tokens, w_qkv, w_out, w_cross, ln_gain, ln_bias, queries):
        T, D = tokens.shape
        NQ = queries.shape[0]
        hcols = D // Q
        Z = S // 4
        G = D // PAIR
        own_rows = NQ // S
        any_spec = pl.BlockSpec(memory_space=pl.ANY)
        vmem_spec = pl.BlockSpec(memory_space=pltpu.VMEM)
        dma = pltpu.SemaphoreType.DMA
        n = S * Q
        results = pl.pallas_call(
            functools.partial(kernel, S, Q, NQ),
            out_shape=(
                jax.ShapeDtypeStruct((T, D), BF16),
                jax.ShapeDtypeStruct((own_rows, D), BF16),
            ),
            in_specs=[any_spec] * 4 + [vmem_spec] * 2 + [any_spec],
            out_specs=(vmem_spec, vmem_spec),
            scratch_shapes=[
                pltpu.VMEM((D, 3 * hcols), BF16),
                pltpu.VMEM((Q * T, D), BF16),
                pltpu.VMEM((3, Q * T, hcols), F32),
                pltpu.VMEM((3, Q * T, hcols), BF16),
                pltpu.VMEM((D, D), BF16),
                pltpu.VMEM((G, D, 2 * PAIR), BF16),
                pltpu.VMEM((NQ, PAIR), BF16),
                pltpu.VMEM((Q, T, hcols), BF16),
                pltpu.VMEM((Q, T, hcols), BF16),
                pltpu.VMEM((T, D), F32),
                pltpu.VMEM((G, T, 2 * PAIR), BF16),
                pltpu.VMEM((G * T, 2 * PAIR), BF16),
                pltpu.VMEM((S, own_rows, PAIR), BF16),
                pltpu.VMEM((S, 8, PAIR), F32),
                pltpu.VMEM((n, own_rows, PAIR), BF16),
                pltpu.VMEM((n, 8, PAIR), F32),
                dma((6 + 2 * G,)),
                dma((Z,)), dma((Z,)), dma((Z,)), dma((Z,)), dma((Z,)), dma((2 * Z,)), dma((2 * Z,)),
                dma((Q,)), dma((Q,)), dma((Q, hcols // PAIR)), dma((Q, hcols // PAIR)), dma((G,)), dma((G,)),
                dma((n,)), dma((n,)), dma((n,)), dma((n,)),
            ],
            compiler_params=pltpu.CompilerParams(
                collective_id=0, has_side_effects=True, vmem_limit_bytes=56 << 20
            ),
        )(tokens, w_qkv, w_out, w_cross, ln_gain.reshape(1, D), ln_bias.reshape(1, D), queries)
        return pl.pallas_call(
            hand_over,
            out_shape=tuple(jax.ShapeDtypeStruct(r.shape, r.dtype) for r in results),
            in_specs=[vmem_spec] * 2,
            out_specs=(vmem_spec, vmem_spec),
        )(*results)

    in_specs = (P(("span", "seq"), None), P("span", None), P(), P(), P(), P(), P())
    out_specs = (P(("span", "seq"), None), P("span", None))
    return jax.shard_map(
        per_device, mesh=mesh, in_specs=in_specs, out_specs=out_specs, check_vma=False
    )
```
